32 devices in a mesh: dp: 16 (over z, x, core), ctx: 2 (over y).
Axes of the slice: x: 2, y: 2, z: 4, core: 2. Of those that a mesh axis runs over, the one named last changes fastest.
Arguments:
- tokens: bfloat16 [4096, 2048], P(('dp', 'ctx')), may hold values from -6 to 6
- cotangent: bfloat16 [4096, 2048], P(('dp', 'ctx')), may hold values from -6 to 6
- projection_weight: float32 [1, 2048, 1536], P(None, ('dp', 'ctx')), may hold values from -0.125 to 0.125
- out_weight: float32 [1, 1024, 2048], P(None, ('dp', 'ctx')), may hold values from -0.75 to 0.75
- gateup_weight: float32 [1, 2048, 5632], P(None, ('dp', 'ctx')), may hold values from -0.125 to 0.125
- down_weight: float32 [1, 2816, 2048], P(None, ('dp', 'ctx')), may hold values from -0.109375 to 0.109375
- norm_gains: float32 [1, 2048, 2], P(None, ('dp', 'ctx')), may hold values from 0.5 to 1.5
- projection_first_moment: float32 [1, 2048, 1536], P(None, ('dp', 'ctx')), may hold values from -6 to 6
- out_mean: float32 [1, 1024, 2048], P(None, ('dp', 'ctx')), may hold values from -6 to 6
- gateup_mean: float32 [1, 2048, 5632], P(None, ('dp', 'ctx')), may hold values from -6 to 6
- down_mean: float32 [1, 2816, 2048], P(None, ('dp', 'ctx')), may hold values from -6 to 6
- gains_mean: float32 [1, 2048, 2], P(None, ('dp', 'ctx')), may hold values from -6 to 6
- projection_second_moment: float32 [1, 2048, 1536], P(None, ('dp', 'ctx')), may hold values from 1 to 10
- out_square: float32 [1, 1024, 2048], P(None, ('dp', 'ctx')), may hold values from 1 to 10
- gateup_square: float32 [1, 2048, 5632], P(None, ('dp', 'ctx')), may hold values from 1 to 10
- down_square: float32 [1, 2816, 2048], P(None, ('dp', 'ctx')), may hold values from 1 to 10
- gains_square: float32 [1, 2048, 2], P(None, ('dp', 'ctx')), may hold values from 1 to 10
Outputs:
- block_output: float32 [4096, 2048], P(('dp', 'ctx'))
- input_grad: float32 [4096, 2048], P(('dp', 'ctx'))
- qkv_grad: float32 [1, 2048, 1536], P(None, ('dp', 'ctx'))
- out_grad: float32 [1, 1024, 2048], P(None, ('dp', 'ctx'))
- gateup_grad: float32 [1, 2048, 5632], P(None, ('dp', 'ctx'))
- down_grad: float32 [1, 2816, 2048], P(None, ('dp', 'ctx'))
- gains_grad: float32 [1, 2048, 2], P(None, ('dp', 'ctx'))
- qkv_next: float32 [1, 2048, 1536], P(None, ('dp', 'ctx'))
- out_next: float32 [1, 1024, 2048], P(None, ('dp', 'ctx'))
- gateup_next: float32 [1, 2048, 5632], P(None, ('dp', 'ctx'))
- down_next: float32 [1, 2816, 2048], P(None, ('dp', 'ctx'))
- gains_next: float32 [1, 2048, 2], P(None, ('dp', 'ctx'))
- qkv_mean_next: float32 [1, 2048, 1536], P(None, ('dp', 'ctx'))
- out_mean_next: float32 [1, 1024, 2048], P(None, ('dp', 'ctx'))
- gateup_mean_next: float32 [1, 2048, 5632], P(None, ('dp', 'ctx'))
- down_mean_next: float32 [1, 2816, 2048], P(None, ('dp', 'ctx'))
- gains_mean_next: float32 [1, 2048, 2], P(None, ('dp', 'ctx'))
- qkv_square_next: float32 [1, 2048, 1536], P(None, ('dp', 'ctx'))
- out_square_next: float32 [1, 1024, 2048], P(None, ('dp', 'ctx'))
- gateup_square_next: float32 [1, 2048, 5632], P(None, ('dp', 'ctx'))
- down_square_next: float32 [1, 2816, 2048], P(None, ('dp', 'ctx'))
- gains_square_next: float32 [1, 2048, 2], P(None, ('dp', 'ctx'))
The draws below stay inside these ranges and needn't reach their ends.
All inputs are finite; a program needn't handle non-finite values.
Results may differ from the reference program's by a relative error of at most 0.019.
Values may be sent and summed in bfloat16 or wider, within the bound.
No kernel may reach another device: no remote copies, remote signals or barrier semaphores. Data moves between devices by JAX's collectives and lax.ppermute only.
A program may use at most 384 MiB of HBM per device.

```python
import math
import jax
import jax.numpy as jnp
from jax import lax

MODEL_WIDTH = 2048
QUERY_HEADS = 16
KEY_VALUE_HEADS = 4
HEAD_SIZE = 64
FF = 2816
DECODER_LAYERS = 1
STEP = 4
TOK_DEV = 128
TOKENS = 4096
N_DP = 16
N_CTX = 2


def block_levels(own_key, dims, shards, low, top_value):
    factor_of = 1.0
    for position, parts in shards:
        draws = jax.random.uniform(jax.random.fold_in(jax.random.fold_in(own_key, 6), position), (parts,), jnp.float32, low / len(shards), top_value / len(shards))
        factor_of = factor_of * jnp.repeat(jnp.exp(draws), dims[position] // parts).reshape((-1,) + (1,) * (len(dims) - 1 - position))
    return factor_of


def noise(rng, extent, scale, limit, pieces=(), held_as=jnp.bfloat16):
    drawn = scale * jax.random.normal(rng, extent, jnp.float32)
    if pieces:
        drawn = drawn * block_levels(rng, extent, pieces, -0.22, 0.18)
    return jnp.clip(drawn, -limit, limit).astype(held_as)


def setup_inputs(seed: int = 0) -> dict:
    key_list = jax.random.split(jax.random.key(seed), 18)
    tokens = noise(key_list[0], (TOKENS, MODEL_WIDTH), 1.0, 6.0, ((0, 32),))
    cotangent = noise(key_list[1], (TOKENS, MODEL_WIDTH), 1.0, 6.0, ((0, 32),))
    projection_weight = noise(key_list[2], (DECODER_LAYERS, MODEL_WIDTH, (QUERY_HEADS + 2 * KEY_VALUE_HEADS) * HEAD_SIZE), MODEL_WIDTH ** -0.5, 0.125, ((1, 32),), jnp.float32)
    out_weight = noise(key_list[3], (DECODER_LAYERS, QUERY_HEADS * HEAD_SIZE, MODEL_WIDTH), (QUERY_HEADS * HEAD_SIZE // 16) ** -0.5, 0.75, ((1, 32),), jnp.float32)
    gateup_weight = noise(key_list[4], (DECODER_LAYERS, MODEL_WIDTH, 2 * FF), MODEL_WIDTH ** -0.5, 0.125, ((1, 32),), jnp.float32)
    down_weight = noise(key_list[5], (DECODER_LAYERS, FF, MODEL_WIDTH), FF ** -0.5, 0.109375, ((1, 32),), jnp.float32)
    norm_gains = jnp.clip(1.0 + 0.1 * jax.random.normal(key_list[6], (DECODER_LAYERS, MODEL_WIDTH, 2), jnp.float32), 0.5, 1.5)
    projection_first_moment = noise(key_list[7], (DECODER_LAYERS, MODEL_WIDTH, (QUERY_HEADS + 2 * KEY_VALUE_HEADS) * HEAD_SIZE), 1.0, 6.0, ((1, 32),), jnp.float32)
    out_mean = noise(key_list[8], (DECODER_LAYERS, QUERY_HEADS * HEAD_SIZE, MODEL_WIDTH), 1.0, 6.0, ((1, 32),), jnp.float32)
    gateup_mean = noise(key_list[9], (DECODER_LAYERS, MODEL_WIDTH, 2 * FF), 1.0, 6.0, ((1, 32),), jnp.float32)
    down_mean = noise(key_list[10], (DECODER_LAYERS, FF, MODEL_WIDTH), 1.0, 6.0, ((1, 32),), jnp.float32)
    gains_mean = noise(key_list[11], (DECODER_LAYERS, MODEL_WIDTH, 2), 1.0, 6.0, ((1, 32),), jnp.float32)
    projection_second_moment = jnp.clip(jnp.exp(math.log(10.0) - 2.3025851 * jax.random.uniform(key_list[12], (DECODER_LAYERS, MODEL_WIDTH, (QUERY_HEADS + 2 * KEY_VALUE_HEADS) * HEAD_SIZE), jnp.float32) ** block_levels(key_list[12], (DECODER_LAYERS, MODEL_WIDTH, (QUERY_HEADS + 2 * KEY_VALUE_HEADS) * HEAD_SIZE), ((1, 32),), -0.2, 0.2)), 1.0, 10.0)
    out_square = jnp.clip(jnp.exp(math.log(10.0) - 2.3025851 * jax.random.uniform(key_list[13], (DECODER_LAYERS, QUERY_HEADS * HEAD_SIZE, MODEL_WIDTH), jnp.float32) ** block_levels(key_list[13], (DECODER_LAYERS, QUERY_HEADS * HEAD_SIZE, MODEL_WIDTH), ((1, 32),), -0.2, 0.2)), 1.0, 10.0)
    gateup_square = jnp.clip(jnp.exp(math.log(10.0) - 2.3025851 * jax.random.uniform(key_list[14], (DECODER_LAYERS, MODEL_WIDTH, 2 * FF), jnp.float32) ** block_levels(key_list[14], (DECODER_LAYERS, MODEL_WIDTH, 2 * FF), ((1, 32),), -0.2, 0.2)), 1.0, 10.0)
    down_square = jnp.clip(jnp.exp(math.log(10.0) - 2.3025851 * jax.random.uniform(key_list[15], (DECODER_LAYERS, FF, MODEL_WIDTH), jnp.float32) ** block_levels(key_list[15], (DECODER_LAYERS, FF, MODEL_WIDTH), ((1, 32),), -0.2, 0.2)), 1.0, 10.0)
    gains_square = jnp.clip(jnp.exp(math.log(10.0) - 2.3025851 * jax.random.uniform(key_list[16], (DECODER_LAYERS, MODEL_WIDTH, 2), jnp.float32) ** block_levels(key_list[16], (DECODER_LAYERS, MODEL_WIDTH, 2), ((1, 32),), -0.2, 0.2)), 1.0, 10.0)
    return dict(tokens=tokens, cotangent=cotangent, projection_weight=projection_weight, out_weight=out_weight, gateup_weight=gateup_weight, down_weight=down_weight, norm_gains=norm_gains, projection_first_moment=projection_first_moment, out_mean=out_mean, gateup_mean=gateup_mean, down_mean=down_mean, gains_mean=gains_mean, projection_second_moment=projection_second_moment, out_square=out_square, gateup_square=gateup_square, down_square=down_square, gains_square=gains_square)


norm_eps = 1e-05
rope_base = 10000.0
beta_one = 0.9
beta_two = 0.99
adam_eps = 1e-08
matrix_rate = 0.01
gain_rate = 0.1
decay_rate = 0.1
masked_score = -1e+30

def dot_rows(left, right):
    return lax.dot_general(left, right, (((0,), (0,)), ((), ())), preferred_element_type=jnp.float32)

def dot_back(left, right):
    return lax.dot_general(left, right, (((1,), (1,)), ((), ())), preferred_element_type=jnp.float32)

def rope_tables(positions):
    half_dim = HEAD_SIZE // 2
    inv_freq = rope_base ** (-(2.0 * jnp.arange(half_dim, dtype=jnp.float32)) / HEAD_SIZE)
    angles = positions.astype(jnp.float32)[:, None] * inv_freq[None, :]
    return (jnp.cos(angles)[:, None, :], jnp.sin(angles)[:, None, :])

def rotate(tensor, cos_table, sin_table, sign_value):
    count_of_rows = tensor.shape[0]
    shaped = tensor.reshape(count_of_rows, -1, HEAD_SIZE)
    half_dim = HEAD_SIZE // 2
    front_half = shaped[..., :half_dim]
    back_half = shaped[..., half_dim:]
    turned = jnp.concatenate([front_half * cos_table - sign_value * back_half * sin_table, back_half * cos_table + sign_value * front_half * sin_table], axis=-1)
    return turned.reshape(count_of_rows, -1)

def normalize(stream):
    inv_rms = lax.rsqrt(lax.optimization_barrier(jnp.mean(stream * stream, axis=-1, keepdims=True)) + norm_eps)
    return (stream * inv_rms, inv_rms)

def normalize_back(gradient, unit_rows, inv_rms, gain_vec):
    scaled = gradient * gain_vec
    back = inv_rms * (scaled - unit_rows * lax.optimization_barrier(jnp.mean(scaled * unit_rows, axis=-1, keepdims=True)))
    return (back, lax.optimization_barrier(jnp.sum(gradient * unit_rows, axis=0)))

def score_block(query_rows, key_rows, query_pos, key_pos):
    count_of_rows = query_rows.shape[0]
    grouped_heads = query_rows.reshape(count_of_rows, KEY_VALUE_HEADS, QUERY_HEADS // KEY_VALUE_HEADS, HEAD_SIZE).astype(jnp.float32)
    key_head_rows = key_rows.reshape(key_rows.shape[0], KEY_VALUE_HEADS, HEAD_SIZE).astype(jnp.float32)
    raw_scores = jnp.einsum('tgjd,sgd->gjts', grouped_heads, key_head_rows) * HEAD_SIZE ** (-0.5)
    allowed = query_pos[:, None] >= key_pos[None, :]
    return jnp.where(allowed[None, None], raw_scores, masked_score)

def attend(query_rows, key_rows, value_rows, query_pos, key_pos):
    scores = score_block(query_rows, key_rows, query_pos, key_pos)
    row_top = lax.optimization_barrier(jnp.max(scores, axis=-1, keepdims=True))
    log_total = row_top + jnp.log(lax.optimization_barrier(jnp.sum(jnp.exp(scores - row_top), axis=-1, keepdims=True)))
    prob_bf = jnp.exp(scores - log_total).astype(jnp.bfloat16)
    value_head_rows = value_rows.reshape(value_rows.shape[0], KEY_VALUE_HEADS, HEAD_SIZE).astype(jnp.float32)
    attention_blend = jnp.einsum('gjts,sgd->tgjd', prob_bf.astype(jnp.float32), value_head_rows)
    return (attention_blend.reshape(query_rows.shape[0], QUERY_HEADS * HEAD_SIZE).astype(jnp.bfloat16), log_total)

def attend_back(query_rows, key_rows, value_rows, attention_blend, blend_gradient, log_total, query_pos, key_pos):
    count_of_rows = query_rows.shape[0]
    scores = score_block(query_rows, key_rows, query_pos, key_pos)
    probs_full = jnp.exp(scores - log_total)
    prob_bf = probs_full.astype(jnp.bfloat16)
    grouped_gradient = blend_gradient.reshape(count_of_rows, KEY_VALUE_HEADS, QUERY_HEADS // KEY_VALUE_HEADS, HEAD_SIZE).astype(jnp.float32)
    grouped_blend = attention_blend.reshape(count_of_rows, KEY_VALUE_HEADS, QUERY_HEADS // KEY_VALUE_HEADS, HEAD_SIZE).astype(jnp.float32)
    grouped_query_rows = query_rows.reshape(count_of_rows, KEY_VALUE_HEADS, QUERY_HEADS // KEY_VALUE_HEADS, HEAD_SIZE).astype(jnp.float32)
    value_head_rows = value_rows.reshape(value_rows.shape[0], KEY_VALUE_HEADS, HEAD_SIZE).astype(jnp.float32)
    key_head_rows = key_rows.reshape(key_rows.shape[0], KEY_VALUE_HEADS, HEAD_SIZE).astype(jnp.float32)
    value_gradient = jnp.einsum('gjts,tgjd->sgd', prob_bf.astype(jnp.float32), grouped_gradient)
    d_prob = jnp.einsum('tgjd,sgd->gjts', grouped_gradient, value_head_rows)
    row_delta = jnp.einsum('tgjd,tgjd->gjt', grouped_gradient, grouped_blend)[..., None]
    d_score = (probs_full * (d_prob - row_delta) * HEAD_SIZE ** (-0.5)).astype(jnp.bfloat16).astype(jnp.float32)
    query_gradient = jnp.einsum('gjts,sgd->tgjd', d_score, key_head_rows)
    key_gradient = jnp.einsum('gjts,tgjd->sgd', d_score, grouped_query_rows)
    return (query_gradient.reshape(count_of_rows, QUERY_HEADS * HEAD_SIZE), key_gradient.reshape(key_rows.shape[0], KEY_VALUE_HEADS * HEAD_SIZE), value_gradient.reshape(key_rows.shape[0], KEY_VALUE_HEADS * HEAD_SIZE))

def forward_layer(stream, weights, positions, cos_table, sin_table):
    w_qkv, w_out, w_gateup, w_down, gain_pair = weights
    gain_pair = gain_pair.astype(jnp.float32)
    q_width = QUERY_HEADS * HEAD_SIZE
    key_stop = (QUERY_HEADS + KEY_VALUE_HEADS) * HEAD_SIZE
    unit_one, inv_one = normalize(stream)
    normed_one = (unit_one * gain_pair[:, 0]).astype(jnp.bfloat16)
    projected = jnp.dot(normed_one, w_qkv, preferred_element_type=jnp.float32)
    query_rows = rotate(projected[:, :q_width], cos_table, sin_table, 1.0).astype(jnp.bfloat16)
    key_rows = rotate(projected[:, q_width:key_stop], cos_table, sin_table, 1.0).astype(jnp.bfloat16)
    value_rows = projected[:, key_stop:].astype(jnp.bfloat16)
    attention_blend, log_total = attend(query_rows, key_rows, value_rows, positions, positions)
    middle = stream + jnp.dot(attention_blend, w_out, preferred_element_type=jnp.float32)
    unit_two, inv_two = normalize(middle)
    normed_two = (unit_two * gain_pair[:, 1]).astype(jnp.bfloat16)
    gateup = jnp.dot(normed_two, w_gateup, preferred_element_type=jnp.float32)
    hidden = (jax.nn.silu(gateup[:, :FF]) * gateup[:, FF:]).astype(jnp.bfloat16)
    result = middle + jnp.dot(hidden, w_down, preferred_element_type=jnp.float32)
    return (result, (unit_one, inv_one, normed_one, query_rows, key_rows, value_rows, attention_blend, log_total, unit_two, inv_two, normed_two, gateup, hidden))

def backward_layer(gradient, weights, kept_state, positions, cos_table, sin_table):
    w_qkv, w_out, w_gateup, w_down, gain_pair = weights
    gain_pair = gain_pair.astype(jnp.float32)
    unit_one, inv_one, normed_one, query_rows, key_rows, value_rows, attention_blend, log_total, unit_two, inv_two, normed_two, gateup, hidden = kept_state
    grad_bf = gradient.astype(jnp.bfloat16)
    d_down_w = dot_rows(hidden, grad_bf)
    d_hidden = dot_back(grad_bf, w_down)
    gate_value = gateup[:, :FF]
    up_value = gateup[:, FF:]
    sigmoid_gate = jax.nn.sigmoid(gate_value)
    d_gate = d_hidden * up_value * sigmoid_gate * (1.0 + gate_value * (1.0 - sigmoid_gate))
    d_up = d_hidden * gate_value * sigmoid_gate
    d_gateup = jnp.concatenate([d_gate, d_up], axis=1).astype(jnp.bfloat16)
    d_gateup_w = dot_rows(normed_two, d_gateup)
    d_normed_two = dot_back(d_gateup, w_gateup)
    d_mid_norm, gain_two = normalize_back(d_normed_two, unit_two, inv_two, gain_pair[:, 1])
    d_middle = gradient + d_mid_norm
    d_mid_bf = d_middle.astype(jnp.bfloat16)
    d_out_w = dot_rows(attention_blend, d_mid_bf)
    blend_gradient = dot_back(d_mid_bf, w_out).astype(jnp.bfloat16)
    query_gradient, key_gradient, value_gradient = attend_back(query_rows, key_rows, value_rows, attention_blend, blend_gradient, log_total, positions, positions)
    query_gradient = rotate(query_gradient, cos_table, sin_table, -1.0)
    key_gradient = rotate(key_gradient, cos_table, sin_table, -1.0)
    d_qkv = jnp.concatenate([query_gradient, key_gradient, value_gradient], axis=1).astype(jnp.bfloat16)
    d_qkv_w = dot_rows(normed_one, d_qkv)
    d_normed_one = dot_back(d_qkv, w_qkv)
    d_in_norm, gain_one = normalize_back(d_normed_one, unit_one, inv_one, gain_pair[:, 0])
    d_stream = d_middle + d_in_norm
    d_gains = jnp.stack([gain_one, gain_two], axis=1)
    return (d_stream, (d_qkv_w, d_out_w, d_gateup_w, d_down_w, d_gains))

def adamw_update(weight, mean_state, square_state, gradient, step_rate, decay_value):
    mean_next = beta_one * mean_state + (1.0 - beta_one) * gradient
    square_next = beta_two * square_state + (1.0 - beta_two) * gradient * gradient
    mean_hat = mean_next / (1.0 - beta_one ** STEP)
    square_hat = square_next / (1.0 - beta_two ** STEP)
    weight_next = weight - step_rate * (mean_hat / (jnp.sqrt(square_hat) + adam_eps) + decay_value * weight)
    return (weight_next, mean_next, square_next)

def reference(tokens, cotangent, projection_weight, out_weight, gateup_weight, down_weight, norm_gains, projection_first_moment, out_mean, gateup_mean, down_mean, gains_mean, projection_second_moment, out_square, gateup_square, down_square, gains_square):
    masters = (projection_weight, out_weight, gateup_weight, down_weight, norm_gains)
    rounded = tuple((master.astype(jnp.bfloat16) for master in masters))
    seq_length = TOK_DEV * N_CTX
    positions = jnp.arange(seq_length, dtype=jnp.int32)
    cos_table, sin_table = rope_tables(positions)

    def per_sequence(totals, seq_pair):
        seq_tokens, seq_cot = seq_pair
        stream = seq_tokens.astype(jnp.float32)
        kept_list = []
        for layer_index in range(DECODER_LAYERS):
            weights = tuple((member[layer_index] for member in rounded))
            stream, kept_state = forward_layer(stream, weights, positions, cos_table, sin_table)
            kept_list.append(kept_state)
        gradient = seq_cot.astype(jnp.float32)
        layer_grads = [None] * DECODER_LAYERS
        for layer_index in reversed(range(DECODER_LAYERS)):
            weights = tuple((member[layer_index] for member in rounded))
            gradient, layer_grads[layer_index] = backward_layer(gradient, weights, kept_list[layer_index], positions, cos_table, sin_table)
        stacked = tuple((jnp.stack([layer_grads[layer_index][member_index] for layer_index in range(DECODER_LAYERS)]) for member_index in range(5)))
        totals = tuple((total + extra for total, extra in zip(totals, stacked)))
        return (totals, (stream, gradient))
    zero_grads = tuple((jnp.zeros(master.shape, jnp.float32) for master in masters))
    seq_tokens = tokens.reshape(N_DP, seq_length, MODEL_WIDTH)
    seq_cots = cotangent.reshape(N_DP, seq_length, MODEL_WIDTH)
    grads, (outputs, input_grads) = lax.scan(per_sequence, zero_grads, (seq_tokens, seq_cots))
    means = (projection_first_moment, out_mean, gateup_mean, down_mean, gains_mean)
    squares = (projection_second_moment, out_square, gateup_square, down_square, gains_square)
    updated = []
    for member_index in range(5):
        step_rate = gain_rate if member_index == 4 else matrix_rate
        decay_value = 0.0 if member_index == 4 else decay_rate
        updated.append(adamw_update(masters[member_index], means[member_index], squares[member_index], grads[member_index], step_rate, decay_value))
    return (outputs.reshape(N_DP * seq_length, MODEL_WIDTH), input_grads.reshape(N_DP * seq_length, MODEL_WIDTH), grads[0], grads[1], grads[2], grads[3], grads[4], updated[0][0], updated[1][0], updated[2][0], updated[3][0], updated[4][0], updated[0][1], updated[1][1], updated[2][1], updated[3][1], updated[4][1], updated[0][2], updated[1][2], updated[2][2], updated[3][2], updated[4][2])
```

```python
import jax
import jax.numpy as jnp
from jax import lax
from jax.sharding import Mesh
from jax.sharding import PartitionSpec as P

QUERY_HEADS = 16
KEY_VALUE_HEADS = 4
HEAD_SIZE = 64
STEP = 4

norm_eps = 1e-05
rope_base = 10000.0
beta_one = 0.9
beta_two = 0.99
adam_eps = 1e-08
matrix_rate = 0.01
gain_rate = 0.1
decay_rate = 0.1
masked_score = -1e30


bf16 = jnp.bfloat16
f32 = jnp.float32
SWAP = [(0, 1), (1, 0)]


def pick(mine, other, index, axis):
    shape = [1] * mine.ndim
    shape[axis] = 2
    place = lax.broadcasted_iota(jnp.int32, shape, axis)
    return jnp.where(place == index, mine, other)


def take(tensor, index, axis):
    return lax.dynamic_slice_in_dim(tensor, index, 1, axis)


def swap(tensor, name):
    return lax.ppermute(tensor, name, SWAP)


def pair_order(mine, other, index, axis):
    return jnp.where(
        index == 0,
        jnp.concatenate([mine, other], axis=axis),
        jnp.concatenate([other, mine], axis=axis),
    )


def gather(tensor, name, axis):
    count = lax.axis_size(name)
    index = lax.axis_index(name)
    if count == 1:
        return tensor
    if count == 2:
        return pick(tensor, swap(tensor, name), index, axis)
    if count == 4:
        near = pick(
            tensor, lax.ppermute(tensor, name, [(0, 1), (1, 0), (2, 3), (3, 2)]), index % 2, axis
        )
        middle = lax.ppermute(near, name, [(1, 2), (2, 1)])
        outer = lax.ppermute(middle, name, [(1, 0), (2, 3)])
        far = jnp.where((index == 1) | (index == 2), middle, outer)
        both = pick(
            jnp.expand_dims(near, axis), jnp.expand_dims(far, axis), index // 2, axis
        )
        shape = list(tensor.shape)
        shape[axis] = 4
        return both.reshape(shape)
    return lax.all_gather(tensor, name, axis=axis, tiled=True)


def gather_chain(tensor, name, axis):
    count = lax.axis_size(name)
    index = lax.axis_index(name)
    if count <= 2:
        return gather(tensor, name, axis)
    below, above = [tensor], [tensor]
    for hop in range(1, count):
        below.append(
            lax.ppermute(below[-1], name, [(i, i + 1) for i in range(hop - 1, count - 1)])
        )
        above.append(
            lax.ppermute(above[-1], name, [(i, i - 1) for i in range(1, count - hop + 1)])
        )
    blocks = []
    for place in range(count):
        block = tensor
        for owner in range(count):
            if owner != place:
                piece = below[owner - place] if place < owner else above[place - owner]
                block = jnp.where(index == owner, piece, block)
        blocks.append(block)
    return jnp.concatenate(blocks, axis=axis)


def add(left, right):
    return left.astype(f32) + right.astype(f32)


def scatter(tensor, name, axis):
    count = lax.axis_size(name)
    index = lax.axis_index(name)
    if count == 1:
        return tensor.astype(f32)
    if count == 2:
        other = swap(take(tensor, 1 - index, axis).astype(bf16), name)
        return add(take(tensor, index, axis), other)
    if count == 4:
        half = index // 2
        near = lax.dynamic_slice_in_dim(tensor, 2 * half, 2, axis)
        far = lax.dynamic_slice_in_dim(tensor, 2 - 2 * half, 2, axis)
        far = add(far, lax.ppermute(far.astype(bf16), name, [(0, 1), (3, 2)])).astype(bf16)
        near = add(near, lax.ppermute(far, name, [(1, 2), (2, 1)]))
        other = lax.ppermute(
            take(near, 1 - index % 2, axis).astype(bf16), name, [(0, 1), (1, 0), (2, 3), (3, 2)]
        )
        return add(take(near, index % 2, axis), other)
    return lax.psum_scatter(
        tensor.astype(bf16), name, scatter_dimension=axis, tiled=True
    ).astype(f32)


def scatter_chain(tensor, name, axis):
    count = lax.axis_size(name)
    index = lax.axis_index(name)
    if count <= 2:
        return scatter(tensor, name, axis)
    total = take(tensor, index, axis)
    for sign in (1, -1):
        arrived = None
        for distance in range(count - 1, 0, -1):
            block = take(tensor, jnp.clip(index + sign * distance, 0, count - 1), axis)
            if arrived is not None:
                block = add(block, arrived)
            hops = [(i, i + 1) for i in range(count - distance)]
            if sign < 0:
                hops = [(count - 1 - i, count - 1 - j) for i, j in hops]
            arrived = lax.ppermute(block.astype(bf16), name, hops)
        total = add(total, arrived)
    return total


def exchange(tensor, name, axis):
    count = lax.axis_size(name)
    index = lax.axis_index(name)
    if count == 1:
        return tensor
    if count == 2:
        other = swap(take(tensor, 1 - index, axis), name)
        return pick(take(tensor, index, axis), other, index, axis)
    return lax.all_to_all(tensor, name, axis, axis, tiled=True)


def dot(left, right):
    return jnp.dot(left, right, preferred_element_type=f32)


def dot_rows(left, right):
    return lax.dot_general(left, right, (((0,), (0,)), ((), ())), preferred_element_type=f32)


def dot_back(left, right):
    return lax.dot_general(left, right, (((1,), (1,)), ((), ())), preferred_element_type=f32)


def rope_tables(positions):
    half_dim = HEAD_SIZE // 2
    inv_freq = rope_base ** (-(2.0 * jnp.arange(half_dim, dtype=f32)) / HEAD_SIZE)
    angles = positions.astype(f32)[:, None] * inv_freq[None, :]
    return (jnp.cos(angles)[:, None, :], jnp.sin(angles)[:, None, :])


def rotate(tensor, cos_table, sin_table, sign_value):
    rows = tensor.shape[0]
    shaped = tensor.reshape(rows, -1, HEAD_SIZE)
    half_dim = HEAD_SIZE // 2
    front = shaped[..., :half_dim]
    back = shaped[..., half_dim:]
    turned = jnp.concatenate(
        [
            front * cos_table - sign_value * back * sin_table,
            back * cos_table + sign_value * front * sin_table,
        ],
        axis=-1,
    )
    return turned.reshape(rows, -1)


def normalize(stream):
    inv_rms = lax.rsqrt(jnp.mean(stream * stream, axis=-1, keepdims=True) + norm_eps)
    return (stream * inv_rms, inv_rms)


def normalize_back(gradient, unit_rows, inv_rms, gain_vec):
    scaled = gradient * gain_vec
    back = inv_rms * (scaled - unit_rows * jnp.mean(scaled * unit_rows, axis=-1, keepdims=True))
    return (back, jnp.sum(gradient * unit_rows, axis=0))


def adamw_update(weight, mean_state, square_state, gradient, step_rate, decay_value):
    mean_next = beta_one * mean_state + (1.0 - beta_one) * gradient
    square_next = beta_two * square_state + (1.0 - beta_two) * gradient * gradient
    mean_hat = mean_next / (1.0 - beta_one**STEP)
    square_hat = square_next / (1.0 - beta_two**STEP)
    weight_next = weight - step_rate * (
        mean_hat / (jnp.sqrt(square_hat) + adam_eps) + decay_value * weight
    )
    return (weight_next, mean_next, square_next)


def shards(
    tokens,
    cotangent,
    projection_weight,
    out_weight,
    gateup_weight,
    down_weight,
    norm_gains,
    projection_first_moment,
    out_mean,
    gateup_mean,
    down_mean,
    gains_mean,
    projection_second_moment,
    out_square,
    gateup_square,
    down_square,
    gains_square,
):
    nz, nx, nc, ny = (lax.axis_size(a) for a in "zxcy")
    core = lax.axis_index("c")
    ctx = lax.axis_index("y")
    other_core = 1 - core
    toks, width = tokens.shape
    half_width = width // 2
    qtr = half_width // 2
    q_half = QUERY_HEADS * HEAD_SIZE // 2
    kv_half = KEY_VALUE_HEADS * HEAD_SIZE // 2
    q_width, kv_width = 2 * q_half, 2 * kv_half
    att_half = q_half + 2 * kv_half
    col_a = att_half // 2
    rows_w = projection_weight.shape[1]
    rows_o = out_weight.shape[1]
    rows_d = down_weight.shape[1]
    hidden_width = gateup_weight.shape[2] // 2
    ff_dev = nz * rows_d
    group = nx * nc * ny
    AX_Z, AX_X, AX_C, AX_Y = 0, 1, 2, 3

    token_pair = jnp.concatenate([tokens, swap(tokens, "c")], axis=0)

    def swap_rows(pair_rows):
        arrived = swap(pair_rows, "c")
        return jnp.concatenate([arrived[toks:], arrived[:toks]], axis=0)

    wqkv = projection_weight[0].astype(bf16)
    pad_rows = 8
    gains_own = norm_gains[0].astype(bf16).T.reshape(1, 2 * rows_w)
    gains_rows = jnp.zeros((pad_rows, col_a), bf16)
    gains_rows = lax.dynamic_update_slice(gains_rows, gains_own, (0, 0))

    def half_columns(which):
        return jnp.concatenate(
            [
                lax.dynamic_slice_in_dim(wqkv, which * q_half, q_half, 1),
                lax.dynamic_slice_in_dim(wqkv, q_width + which * kv_half, kv_half, 1),
                lax.dynamic_slice_in_dim(wqkv, q_width + kv_width + which * kv_half, kv_half, 1),
            ],
            axis=1,
        )

    def with_gains(block):
        return jnp.concatenate(
            [block, jnp.concatenate([gains_rows, jnp.zeros_like(gains_rows)], axis=1)], axis=0
        )

    qkv_piece = pick(
        with_gains(half_columns(core))[None],
        swap(with_gains(half_columns(other_core))[None], "c"),
        core,
        0,
    )
    wo = out_weight[0].astype(bf16)
    o_piece = pick(
        lax.dynamic_slice_in_dim(wo, core * half_width, half_width, 1)[None],
        swap(lax.dynamic_slice_in_dim(wo, other_core * half_width, half_width, 1)[None], "c"),
        core,
        0,
    )

    def gather_rows(piece, order):
        block = piece[None, None, :, None]
        for name in order:
            block = gather(block, name, {"z": AX_Z, "x": AX_X, "y": AX_Y}[name])
        return block

    qkv_a = gather_rows(qkv_piece[:, :, :col_a], "zxy")
    qkv_b = gather_rows(qkv_piece[:, :rows_w, col_a:], "zyx")
    w_qkv_a = qkv_a[..., :rows_w, :].reshape(width, col_a)
    w_qkv_b = qkv_b.reshape(width, col_a)
    gain_block = qkv_a[..., rows_w, : 2 * rows_w].reshape(nz, nx, nc, ny, 2, rows_w)
    gain_one = gain_block[..., 0, :].reshape(width).astype(f32)
    gain_two = gain_block[..., 1, :].reshape(width).astype(f32)
    w_o_a = gather_rows(o_piece[:, :, :qtr], "zxy").reshape(q_width, qtr)
    w_o_b = gather_rows(o_piece[:, :, qtr:], "zyx").reshape(q_width, qtr)

    wgu = gateup_weight[0].astype(bf16).reshape(rows_w, 2, nz, nx, nc, ny, rows_d)
    wgu = wgu.transpose(1, 3, 4, 5, 0, 2, 6).reshape(2, nx, nc, ny, rows_w, ff_dev)
    wgu = exchange(wgu, "c", 2)
    gate_piece = exchange(exchange(wgu[0], "x", 0), "y", 2)
    up_piece = exchange(exchange(wgu[1], "y", 2), "x", 0)
    gu_piece = jnp.stack([gate_piece, up_piece]).reshape(2, 1, width // nz, ff_dev)
    w_gu = gather_chain(gu_piece, "z", 1).reshape(2, width, ff_dev)
    w_gate, w_up = w_gu[0], w_gu[1]
    w_down = gather_chain(down_weight.astype(bf16), "z", 0).reshape(ff_dev, width)

    def plane_gather(rows):
        first = rows[None, None, None, : toks // 2]
        second = rows[None, None, None, toks // 2 :]
        first = gather(gather(first, "x", 0), "y", 1)
        second = gather(gather(second, "y", 1), "x", 0)
        both = jnp.stack([first, second])
        return gather(both, "c", 3).reshape(group * toks, width)

    def plane_scatter(partial):
        block = partial.reshape(2, nx, ny, nc, toks // 2, width)
        block = scatter(block, "c", 3)
        first = scatter(scatter(block[0], "y", 1), "x", 0)
        second = scatter(scatter(block[1], "x", 0), "y", 1)
        return jnp.concatenate([first, second], axis=3).reshape(toks, width)

    cot_plane = plane_gather(cotangent)

    own_pos = ctx * toks + jnp.arange(toks, dtype=jnp.int32)
    far_pos = (1 - ctx) * toks + jnp.arange(toks, dtype=jnp.int32)
    key_pos = jnp.concatenate([far_pos, own_pos])
    allowed = (own_pos[:, None] >= key_pos[None, :])[None, None, None]
    cos_table, sin_table = rope_tables(jnp.concatenate([own_pos, own_pos]))

    stream = token_pair.astype(f32)
    unit_one, inv_one = normalize(stream)
    normed_one = (unit_one * gain_one).astype(bf16)
    projected = jnp.concatenate([dot(normed_one, w_qkv_a), dot(normed_one, w_qkv_b)], axis=1)
    query = rotate(projected[:, :q_half], cos_table, sin_table, 1.0).astype(bf16)
    keys = rotate(projected[:, q_half : q_half + kv_half], cos_table, sin_table, 1.0).astype(bf16)
    values = projected[:, q_half + kv_half :].astype(bf16)
    own_kv = jnp.concatenate([keys, values], axis=1)
    far_kv = swap(own_kv, "y")
    groups, per_group = KEY_VALUE_HEADS // 2, QUERY_HEADS // KEY_VALUE_HEADS
    kv = jnp.concatenate(
        [far_kv.reshape(2, toks, 2, groups, HEAD_SIZE), own_kv.reshape(2, toks, 2, groups, HEAD_SIZE)],
        axis=1,
    )
    all_keys, all_values = kv[:, :, 0], kv[:, :, 1]
    query_heads = query.reshape(2, toks, groups, per_group, HEAD_SIZE)
    scores = (
        jnp.einsum("btgjd,bsgd->bgjts", query_heads, all_keys, preferred_element_type=f32)
        * HEAD_SIZE ** (-0.5)
    )
    scores = jnp.where(allowed, scores, masked_score)
    row_top = jnp.max(scores, axis=-1, keepdims=True)
    log_total = row_top + jnp.log(jnp.sum(jnp.exp(scores - row_top), axis=-1, keepdims=True))
    probs = jnp.exp(scores - log_total)
    probs_bf = probs.astype(bf16)
    blend_half = jnp.einsum(
        "bgjts,bsgd->btgjd", probs_bf, all_values, preferred_element_type=f32
    ).astype(bf16)
    blend_half = blend_half.reshape(2 * toks, q_half)
    blend = pair_order(blend_half, swap_rows(blend_half), core, 1)
    attended = jnp.concatenate([dot(blend, w_o_a), dot(blend, w_o_b)], axis=1)
    middle = stream[:toks] + pair_order(attended[:toks], swap(attended[toks:], "c"), core, 1)
    unit_two, inv_two = normalize(middle)
    normed_two = plane_gather((unit_two * gain_two).astype(bf16))

    gate_value = dot(normed_two, w_gate)
    up_value = dot(normed_two, w_up)
    sigmoid_gate = jax.nn.sigmoid(gate_value)
    hidden = (gate_value * sigmoid_gate * up_value).astype(bf16)
    grad_down = dot_rows(hidden, cot_plane).astype(bf16).reshape(nz, rows_d, width)
    d_hidden = dot_back(cot_plane, w_down)
    d_gate = (d_hidden * up_value * sigmoid_gate * (1.0 + gate_value * (1.0 - sigmoid_gate))).astype(
        bf16
    )
    d_up = (d_hidden * gate_value * sigmoid_gate).astype(bf16)
    d_normed_two = plane_scatter((dot_back(d_gate, w_gate) + dot_back(d_up, w_up)).astype(bf16))
    result = middle + plane_scatter(dot(hidden, w_down).astype(bf16))
    grad_gu = jnp.stack([dot_rows(normed_two, d_gate), dot_rows(normed_two, d_up)]).astype(bf16)
    grad_gu = grad_gu.reshape(2, nz, width // nz, ff_dev)
    owned_down = scatter_chain(grad_down, "z", 0)
    owned_gu = scatter_chain(grad_gu, "z", 1).astype(bf16)
    owned_gu = owned_gu.reshape(2, nx, nc, ny, rows_w, ff_dev)
    owned_gate = exchange(exchange(owned_gu[0], "y", 2), "x", 0)
    owned_up = exchange(exchange(owned_gu[1], "x", 0), "y", 2)
    owned_gu = exchange(jnp.stack([owned_gate, owned_up]), "c", 2)
    owned_gu = owned_gu.reshape(2, nx, nc, ny, rows_w, nz, rows_d)
    owned_gu = owned_gu.transpose(4, 0, 5, 1, 2, 3, 6).reshape(rows_w, 2 * hidden_width).astype(f32)

    cot_own = cotangent.astype(f32)
    d_mid_norm, gain_two_sum = normalize_back(d_normed_two, unit_two, inv_two, gain_two)
    d_middle = cot_own + d_mid_norm
    d_mid_bf = d_middle.astype(bf16)
    mid_mine = lax.dynamic_slice_in_dim(d_mid_bf, core * half_width, half_width, 1)
    mid_other = lax.dynamic_slice_in_dim(d_mid_bf, other_core * half_width, half_width, 1)
    mid_cols = jnp.concatenate([mid_mine, swap(mid_other, "c")], axis=0)
    mid_a, mid_b = mid_cols[:, :qtr], mid_cols[:, qtr:]
    d_blend_part = dot_back(mid_a, w_o_a) + dot_back(mid_b, w_o_b)
    d_blend = (
        lax.dynamic_slice_in_dim(d_blend_part, core * q_half, q_half, 1)
        + swap_rows(lax.dynamic_slice_in_dim(d_blend_part, other_core * q_half, q_half, 1))
    ).astype(bf16)
    grad_heads = d_blend.reshape(2, toks, groups, per_group, HEAD_SIZE)
    blend_heads = blend_half.reshape(2, toks, groups, per_group, HEAD_SIZE)
    d_values = jnp.einsum("bgjts,btgjd->bsgd", probs_bf, grad_heads, preferred_element_type=f32)
    d_prob = jnp.einsum("btgjd,bsgd->bgjts", grad_heads, all_values, preferred_element_type=f32)
    delta = jnp.einsum(
        "btgjd,btgjd->bgjt", grad_heads, blend_heads, preferred_element_type=f32
    )[..., None]
    d_score = (probs * (d_prob - delta) * HEAD_SIZE ** (-0.5)).astype(bf16)
    d_query = jnp.einsum("bgjts,bsgd->btgjd", d_score, all_keys, preferred_element_type=f32)
    d_keys = jnp.einsum("bgjts,btgjd->bsgd", d_score, query_heads, preferred_element_type=f32)
    d_kv = jnp.concatenate(
        [d_keys.reshape(2, 2 * toks, kv_half), d_values.reshape(2, 2 * toks, kv_half)], axis=2
    )
    d_kv_own = d_kv[:, toks:] + swap(d_kv[:, :toks].astype(bf16), "y").astype(f32)
    d_kv_own = d_kv_own.reshape(2 * toks, 2 * kv_half)
    d_qkv = jnp.concatenate(
        [
            rotate(d_query.reshape(2 * toks, q_half), cos_table, sin_table, -1.0),
            rotate(d_kv_own[:, :kv_half], cos_table, sin_table, -1.0),
            d_kv_own[:, kv_half:],
        ],
        axis=1,
    ).astype(bf16)
    d_normed_part = dot_back(d_qkv[:, :col_a], w_qkv_a) + dot_back(d_qkv[:, col_a:], w_qkv_b)
    d_normed_one = d_normed_part[:toks] + swap(d_normed_part[toks:], "c")
    d_in_norm, gain_one_sum = normalize_back(
        d_normed_one, unit_one[:toks], inv_one[:toks], gain_one
    )
    input_grad = d_middle + d_in_norm

    def scatter_rows(grad, order):
        for name in order:
            grad = scatter(grad, name, {"z": AX_Z, "x": AX_X, "y": AX_Y}[name])
        return grad[0, 0, :, 0]

    def by_rows(grad, rows):
        return grad.astype(bf16).reshape(nz, nx, nc, ny, rows, grad.shape[-1])

    grad_o_a = scatter_rows(by_rows(dot_rows(blend, mid_a), rows_o), "yxz")
    grad_o_b = scatter_rows(by_rows(dot_rows(blend, mid_b), rows_o), "xyz")
    grad_o = jnp.concatenate([grad_o_a, grad_o_b], axis=2)
    owned_o = pair_order(
        take(grad_o, core, 0), swap(take(grad_o, other_core, 0), "c"), core, 2
    )

    gain_sums = jnp.stack(
        [
            gain_one_sum.reshape(nz, nx, nc, ny, rows_w),
            gain_two_sum.reshape(nz, nx, nc, ny, rows_w),
        ],
        axis=4,
    ).reshape(nz, nx, nc, ny, 1, 2 * rows_w)
    gain_sums = jnp.pad(
        gain_sums.astype(bf16), [(0, 0)] * 4 + [(0, pad_rows - 1), (0, col_a - 2 * rows_w)]
    )
    grad_a = jnp.concatenate(
        [by_rows(dot_rows(normed_one, d_qkv[:, :col_a]), rows_w), gain_sums], axis=4
    )
    grad_a = scatter_rows(grad_a, "yxz")
    grad_b = scatter_rows(by_rows(dot_rows(normed_one, d_qkv[:, col_a:]), rows_w), "xyz")
    grad_b = jnp.pad(grad_b, [(0, 0), (0, pad_rows), (0, 0)])
    grad_ab = jnp.concatenate([grad_a, grad_b], axis=2)
    mine, other = take(grad_ab, core, 0)[0], swap(take(grad_ab, other_core, 0), "c")[0]
    gain_total = (mine[rows_w, : 2 * rows_w] + other[rows_w, : 2 * rows_w]).reshape(2, rows_w)
    owned_gains = gain_total.T[None]
    mine, other = mine[:rows_w], other[:rows_w]
    owned_qkv = jnp.concatenate(
        [
            pair_order(mine[:, a:b], other[:, a:b], core, 1)
            for a, b in ((0, q_half), (q_half, q_half + kv_half), (q_half + kv_half, att_half))
        ],
        axis=1,
    )[None]

    grads = (owned_qkv, owned_o, owned_gu, owned_down, owned_gains)
    masters = (projection_weight, out_weight, gateup_weight, down_weight, norm_gains)
    means = (projection_first_moment, out_mean, gateup_mean, down_mean, gains_mean)
    squares = (projection_second_moment, out_square, gateup_square, down_square, gains_square)
    grads = tuple(g.reshape(m.shape) for g, m in zip(grads, masters))
    updated = [
        adamw_update(
            masters[i],
            means[i],
            squares[i],
            grads[i],
            gain_rate if i == 4 else matrix_rate,
            0.0 if i == 4 else decay_rate,
        )
        for i in range(5)
    ]
    return (
        (result, input_grad)
        + grads
        + tuple(u[0] for u in updated)
        + tuple(u[1] for u in updated)
        + tuple(u[2] for u in updated)
    )


def sizes_of(mesh):
    data, pair = mesh.shape["dp"], mesh.shape["ctx"]
    devices = list(mesh.devices.flat)
    cores = len({d.core_on_chip for d in devices})
    depth = len({d.coords[2] for d in devices})
    return (depth, data // (depth * cores), cores, pair)


def solution(mesh):
    split = Mesh(mesh.devices.reshape(sizes_of(mesh)), ("z", "x", "c", "y"))
    every = ("z", "x", "c", "y")
    rows = P(every, None)
    state = P(None, every, None)
    return jax.shard_map(
        shards,
        mesh=split,
        in_specs=(rows, rows) + (state,) * 15,
        out_specs=(rows, rows) + (state,) * 20,
        check_vma=False,
    )
```
